32 devices in a mesh: vocab: 8 (over y, x, core), width: 4 (over z).
Axes of the slice: x: 2, y: 2, z: 4, core: 2. Of those that a mesh axis runs over, the one named last changes fastest.
Arguments:
- hidden: bfloat16 [256, 2880], P('width'), may hold values from -60 to 60
- gain: float32 [2880], replicated, may hold values from 0.1 to 1.9
- unembed: bfloat16 [2880, 50176], P('width', 'vocab'), may hold values from -8 to 8
- targets: int32 [256], replicated, may hold values from 0 to 50175
- seq_ids: int32 [256], replicated, may hold values from 0 to 47, as said below
Outputs:
- log_normalizer: float32 [256], P('width')
- entropy: float32 [256], P('width')
- token_logprob: float32 [256], P('width')
- seq_mean: float32 [48], replicated
The draws below stay inside these ranges and needn't reach their ends.
Inputs may be any that keep to these rules, and one draw needn't show every extreme that they name: `seq_ids`: rows of one sequence are consecutive and ids never fall; every sequence has at least one row.
All inputs are finite; a program needn't handle non-finite values.
Results may differ from the reference program's by a relative error of at most 0.0014.
Values may be sent and summed in bfloat16 or wider, within the bound.
A program may use at most 128 MiB of HBM per device.

```python
import jax
import jax.numpy as jnp
from jax import lax

D = 2880
ROWS_DEV = 64
SEQS = 48
ROWS = 256
VOCAB = 50176


def pattern_vector(key):
    return jax.random.truncated_normal(jax.random.fold_in(key, 71), -3.0, 3.0, (D,), jnp.float32)


def column_at(key):
    return jax.random.randint(jax.random.fold_in(key, 72), (), 0, VOCAB - 1)


def draw_unembed(key, part):
    weights = jax.random.truncated_normal(jax.random.fold_in(key, 3), -6.0, 6.0, (D, VOCAB), jnp.float32) * 0.056
    amplitude = 260.0
    pattern = pattern_vector(key) * (amplitude / D)
    paired = jnp.stack([pattern, pattern * 0.99], axis=1)
    weights = lax.dynamic_update_slice(weights, paired, (jnp.int32(0), column_at(key).astype(jnp.int32)))
    return weights.astype(jnp.bfloat16)


def draw_hidden(key, part):
    base = jax.random.truncated_normal(jax.random.fold_in(key, 5), -6.0, 6.0, (ROWS, D), jnp.float32)
    scales = jnp.exp(jax.random.uniform(jax.random.fold_in(key, 6), (ROWS, 1), jnp.float32, 0.0, 2.3))
    result = base * scales
    pattern = pattern_vector(key)
    row_ids = jnp.arange(ROWS)
    strength = jnp.where(row_ids % 8 == 3, 1.0, jnp.where(row_ids % 8 == 6, 0.85, jnp.where(row_ids % 8 == 1, 0.6, 0.0)))[:, None]
    result = strength * pattern[None, :] * scales + (1.0 - strength) * result
    return result.astype(jnp.bfloat16)


def draw_seq_ids(key, part):
    order = jax.random.permutation(jax.random.fold_in(key, 91), ROWS - 1)
    cuts = order[:SEQS - 1].astype(jnp.int32) + 1
    row_ids = jnp.arange(ROWS, dtype=jnp.int32)
    return jnp.sum((cuts[None, :] <= row_ids[:, None]).astype(jnp.int32), axis=1).astype(jnp.int32)


def plant(entries, stream_key, low, largest):
    place = [jax.random.randint(jax.random.fold_in(stream_key, axis), (), 0, length) for axis, length in enumerate(entries.shape)]
    main_axis = entries.shape.index(max(entries.shape))
    beside = place[:main_axis] + [(place[main_axis] + 1) % entries.shape[main_axis]] + place[main_axis + 1:]
    return entries.at[tuple(place)].set(low).at[tuple(beside)].set(largest)


def setup_inputs(seed: int = 0) -> dict:
    seeds = jax.random.split(jax.random.key(seed), 6)
    return {
        "hidden": draw_hidden(jax.random.fold_in(seeds[5], 71), 0),
        "gain": jnp.clip(1.0 + 0.18 * jax.random.normal(seeds[1], (D,), jnp.float32), 0.1, 1.9),
        "unembed": draw_unembed(jax.random.fold_in(seeds[5], 71), 0),
        "targets": plant(jax.random.randint(seeds[3], (ROWS,), 0, VOCAB), jax.random.fold_in(seeds[3], 1), 0, VOCAB - 1).astype(jnp.int32),
        "seq_ids": draw_seq_ids(jax.random.fold_in(seeds[5], 71), 0),
    }


def reference(hidden, gain, unembed, targets, seq_ids):
    values = hidden.astype(jnp.float32)
    square = lax.optimization_barrier(jnp.mean(values * values, axis=1, keepdims=True))
    normed = (values * lax.rsqrt(square + 1e-05) * gain[None, :]).astype(jnp.bfloat16)
    blocks = ROWS // ROWS_DEV
    normed_blocks = normed.reshape(blocks, ROWS_DEV, D)
    target_blocks = targets.astype(jnp.int32).reshape(blocks, ROWS_DEV)

    def row_block(inputs):
        block_rows, block_targets = inputs
        logits = jnp.dot(block_rows, unembed, preferred_element_type=jnp.float32)
        row_max = lax.optimization_barrier(jnp.max(logits, axis=1))
        shifted = jnp.exp(logits - row_max[:, None])
        exp_total = lax.optimization_barrier(jnp.sum(shifted, axis=1))
        log_norm = row_max + jnp.log(exp_total)
        row_entropy = log_norm - lax.optimization_barrier(jnp.sum(shifted * logits, axis=1)) / exp_total
        target_logit = jnp.take_along_axis(logits, block_targets[:, None], axis=1)[:, 0]
        return (log_norm, row_entropy, target_logit - log_norm)
    log_normalizer, entropy, token_logprob = lax.map(row_block, (normed_blocks, target_blocks))
    log_normalizer = log_normalizer.reshape(ROWS)
    entropy = entropy.reshape(ROWS)
    token_logprob = token_logprob.reshape(ROWS)
    member = (seq_ids[:, None] == jnp.arange(SEQS, dtype=jnp.int32)[None, :]).astype(jnp.float32)
    seq_sums = jnp.dot(token_logprob, member, precision=lax.Precision.HIGHEST)
    seq_counts = lax.optimization_barrier(jnp.sum(member, axis=0))
    return (log_normalizer, entropy, token_logprob, seq_sums / seq_counts)
```

```python
import functools

import jax
import jax.numpy as jnp
from jax import lax
from jax.experimental import pallas as pl
from jax.experimental.pallas import tpu as pltpu
from jax.sharding import PartitionSpec as P

SEQS = 48
LANES = 128
LAG = 7
GROUPS = 2
LOWEST = -1e38
LEVELS = 32760.0
TINY = 1e-30
MESH = pl.DeviceIdType.MESH


def kernel(
    n, nv, hidden_ref, gain_ref, unembed_ref, targets_ref, seq_ref, out_ref,
    weights, blocks, rows_in, buf, part, bound, steps, target_cols, state, packed, gathered, final,
    w_sem, own_sem, x_send, x_recv, p_send, p_recv, c_send, c_recv, b_send, b_recv,
    v_send, v_recv, f_send, f_recv,
):
    me = lax.axis_index("width")
    my_vocab = lax.axis_index("vocab")
    own_rows, width_dim = hidden_ref.shape
    share = width_dim // n
    half = (n // 2) * own_rows
    chunks = unembed_ref.shape[1] // LANES
    last = n - 1
    group_blocks = n // 2 // GROUPS
    group_rows = group_blocks * own_rows
    items = GROUPS * chunks
    slots = last * LAG + 1
    tile = tile_of(chunks)

    early = tile * LANES
    loads = []
    for k, cols in enumerate((pl.ds(0, early), pl.ds(early, chunks * LANES - early))):
        loads.append(
            pltpu.make_async_copy(unembed_ref.at[:, cols], weights.at[:, cols], w_sem.at[k])
        )
        loads[k].start()

    barrier = pltpu.get_barrier_semaphore()
    for k in range(1, n):
        pl.semaphore_signal(
            barrier, inc=1, device_id={"width": lax.rem(me + k, n)}, device_id_type=MESH
        )
    for k in range(1, nv):
        pl.semaphore_signal(
            barrier, inc=1, device_id={"vocab": lax.rem(my_vocab + k, nv)}, device_id_type=MESH
        )

    values = hidden_ref[...].astype(jnp.float32)
    square = jnp.mean(values * values, axis=1, keepdims=True)
    normed = (values * lax.rsqrt(square + 1e-05) * gain_ref[...][None, :]).astype(jnp.bfloat16)
    for j in range(n):
        blocks[j] = normed[:, j * share : (j + 1) * share]

    pl.semaphore_wait(barrier, n - 1 + nv - 1)

    my_part = pl.ds(pl.multiple_of(lax.rem(my_vocab, 2) * (own_rows // 2), own_rows // 2), own_rows // 2)
    other_part = pl.ds(
        pl.multiple_of((1 - lax.rem(my_vocab, 2)) * (own_rows // 2), own_rows // 2), own_rows // 2
    )
    partner = my_vocab + 1 - 2 * lax.rem(my_vocab, 2)

    def row_copy(peer, source):
        return pltpu.make_async_remote_copy(
            src_ref=blocks.at[peer, my_part],
            dst_ref=rows_in.at[source, my_part],
            send_sem=x_send.at[peer],
            recv_sem=x_recv.at[source],
            device_id={"width": peer},
            device_id_type=MESH,
        )

    def pass_rows(source, part):
        return pltpu.make_async_remote_copy(
            src_ref=rows_in.at[source, part],
            dst_ref=rows_in.at[source, part],
            send_sem=p_send.at[source],
            recv_sem=p_recv.at[source],
            device_id={"vocab": partner},
            device_id_type=MESH,
        )

    def send_rows():
        for k in range(1, n):
            row_copy(lax.rem(me + jnp.where(me < n // 2, k, n - k), n), me).start()

    rows_now = jnp.where(me < n // 2, me, last - me) < group_blocks

    @pl.when(rows_now)
    def _():
        send_rows()

    own = pltpu.make_async_copy(blocks.at[me], rows_in.at[me], own_sem)
    own.start()

    target_row = targets_ref[...].astype(jnp.float32)
    target_all = jnp.transpose(jnp.broadcast_to(target_row, (LANES, 2 * half)))
    target_cols[0] = target_all[:half]
    target_cols[1] = target_all[half:]
    state[0] = jnp.full((half, LANES), LOWEST, jnp.float32)
    for k in range(1, 4):
        state[k] = jnp.zeros((half, LANES), jnp.float32)

    own.wait()
    loads[0].wait()

    def chunk_copy(side, c, peer):
        return pltpu.make_async_remote_copy(
            src_ref=buf.at[side, c],
            dst_ref=buf.at[side, c],
            send_sem=c_send.at[side, lax.rem(c, slots)],
            recv_sem=c_recv.at[side, lax.rem(c, slots)],
            device_id={"width": peer},
            device_id_type=MESH,
        )

    first_col = my_vocab * (chunks * LANES)
    lane = lax.broadcasted_iota(jnp.int32, (half, LANES), 1)
    item_lane = lax.broadcasted_iota(jnp.int32, (group_rows, LANES), 1)

    def bound_copy(side, t, peer):
        return pltpu.make_async_remote_copy(
            src_ref=bound.at[side, t],
            dst_ref=bound.at[side, t],
            send_sem=b_send.at[side, t],
            recv_sem=b_recv.at[side, t],
            device_id={"width": peer},
            device_id_type=MESH,
        )

    def by_vreg(values):
        return values.reshape(group_rows // 8, 8, LANES)

    def partial_tile(side, first_block, c, t, head, tail, peer):
        cols = pl.ds(pl.multiple_of(c * LANES, LANES), tile * LANES)
        x = rows_in[pl.ds(first_block, group_blocks)].reshape(group_rows, share)
        logits = jnp.dot(x, weights[:, cols], preferred_element_type=jnp.float32)
        peak = jnp.full((8, LANES), TINY, jnp.float32)
        for j in range(tile):
            piece = logits[:, j * LANES : (j + 1) * LANES]
            part[side, j] = piece
            peak = jnp.maximum(peak, jnp.max(jnp.abs(by_vreg(piece)), axis=0))

        def announce(limit):
            bound[side, t] = limit
            steps[side, 1] = LEVELS / limit
            bound_copy(side, t, peer).start()

        @pl.when(me == head)
        def _():
            announce(peak)

        @pl.when(me != head)
        def _():
            bound_copy(side, t, peer).wait_recv()
            incoming = bound[side, t]
            steps[side, 0] = incoming * (1.0 / LEVELS)

            @pl.when(me != tail)
            def _():
                announce(incoming + peak)

    def to_codes(side, values):
        scaled = by_vreg(values) * steps[side, 1][None]
        return jnp.round(scaled).astype(jnp.int32).astype(jnp.int16).reshape(group_rows, LANES)

    def from_codes(side, codes):
        values = by_vreg(codes.astype(jnp.int32).astype(jnp.float32)) * steps[side, 0][None]
        return values.reshape(group_rows, LANES)

    def take_stats(side, first_block, c, logits):
        rows = pl.ds(pl.multiple_of((first_block - side * (n // 2)) * own_rows, 8), group_rows)
        column = (first_col + c * LANES + item_lane).astype(jnp.float32)
        old_max = state[0, rows]
        new_max = jnp.maximum(old_max, logits)
        scale = jnp.exp(old_max - new_max)
        shifted = jnp.exp(logits - new_max)
        state[0, rows] = new_max
        state[1, rows] = state[1, rows] * scale + shifted
        state[2, rows] = state[2, rows] * scale + shifted * logits
        state[3, rows] = state[3, rows] + jnp.where(column == target_cols[side, rows], logits, 0.0)

    def advance(side, item, head, tail, peer):
        @pl.when((item >= 0) & (item < items))
        def _():
            group = item // chunks
            c = item - group * chunks
            first_block = group * group_blocks if side == 0 else n - (group + 1) * group_blocks
            for g in range(GROUPS):
                start = g * group_blocks if side == 0 else n - (g + 1) * group_blocks

                @pl.when(item == g * (chunks // 2))
                def _():
                    for w in range(start, start + group_blocks):

                        @pl.when(me != w)
                        def _():
                            row_copy(w, w).wait_recv()
                            pass_rows(w, my_part).start()

                @pl.when(item == g * chunks)
                def _():
                    for w in range(start, start + group_blocks):

                        @pl.when(me != w)
                        def _():
                            pass_rows(w, other_part).wait_recv()

            k = lax.rem(item, tile)

            @pl.when(k == 0)
            def _():
                partial_tile(side, first_block, c, item // tile, head, tail, peer)

            @pl.when((me != tail) & (item >= slots))
            def _():
                chunk_copy(side, item - slots, peer).wait_send()

            @pl.when(me == head)
            def _():
                buf[side, item] = to_codes(side, part[side, k])
                chunk_copy(side, item, peer).start()

            @pl.when(me != head)
            def _():
                chunk_copy(side, item, peer).wait_recv()
                total = from_codes(side, buf[side, item]) + part[side, k]

                @pl.when(me != tail)
                def _():
                    buf[side, item] = to_codes(side, total)
                    chunk_copy(side, item, peer).start()

                @pl.when(me == tail)
                def _():
                    take_stats(side, first_block, c, total)

    down = lax.rem(me + n - 1, n)
    up = lax.rem(me + 1, n)

    def step(s, carry):
        @pl.when(s == 1)
        def _():
            loads[1].wait()

        @pl.when((s == 2 * LAG) & jnp.logical_not(rows_now))
        def _():
            send_rows()

        advance(0, s - me * LAG, 0, last, up)
        advance(1, s - (last - me) * LAG, last, 0, down)
        return carry

    lax.fori_loop(0, items + last * LAG, step, 0)

    def stats_copy(peer, source):
        return pltpu.make_async_remote_copy(
            src_ref=packed.at[0],
            dst_ref=gathered.at[source],
            send_sem=v_send.at[peer],
            recv_sem=v_recv.at[source],
            device_id={"vocab": peer},
            device_id_type=MESH,
        )

    def final_copy(side, peer):
        return pltpu.make_async_remote_copy(
            src_ref=packed.at[1],
            dst_ref=final.at[side],
            send_sem=f_send.at[peer],
            recv_sem=f_recv.at[side],
            device_id={"width": peer},
            device_id_type=MESH,
        )

    def finish(side):
        lane_max = state[0]
        row_max = jnp.max(lane_max, axis=1, keepdims=True)
        scale = jnp.exp(lane_max - row_max)
        columns = (
            row_max,
            jnp.sum(state[1] * scale, axis=1, keepdims=True),
            jnp.sum(state[2] * scale, axis=1, keepdims=True),
            jnp.sum(state[3], axis=1, keepdims=True),
        )
        wide = jnp.zeros((half, LANES), jnp.float32)
        for k in range(4):
            wide = jnp.where(lane == k, columns[k], wide)
        flat = jnp.transpose(wide)[:8]
        packed[0] = flat
        for k in range(1, nv):
            stats_copy(lax.rem(my_vocab + k, nv), my_vocab).start()
        gathered[my_vocab] = flat
        for k in range(1, nv):
            peer = lax.rem(my_vocab + k, nv)
            stats_copy(peer, peer).wait_recv()
        parts = [gathered[v] for v in range(nv)]
        top = functools.reduce(jnp.maximum, [part[0:1] for part in parts])
        total = jnp.zeros_like(top)
        weighted = jnp.zeros_like(top)
        target = jnp.zeros_like(top)
        for part in parts:
            factor = jnp.exp(part[0:1] - top)
            total = total + part[1:2] * factor
            weighted = weighted + part[2:3] * factor
            target = target + part[3:4]
        log_normalizer = top + jnp.log(total)
        rows = lax.broadcasted_iota(jnp.int32, (8, half), 0)
        result = jnp.where(
            rows == 0,
            log_normalizer,
            jnp.where(rows == 1, log_normalizer - weighted / total, target - log_normalizer),
        )
        packed[1] = result
        for k in range(1, n):
            final_copy(side, lax.rem(me + k, n)).start()
        final[side] = result

    @pl.when(me == last)
    def _():
        finish(0)

    @pl.when(me == 0)
    def _():
        finish(1)

    @pl.when(me != last)
    def _():
        final_copy(0, 0).wait_recv()

    @pl.when(me != 0)
    def _():
        final_copy(1, 0).wait_recv()

    ids = lax.broadcasted_iota(jnp.int32, (LANES, half), 0)
    sums = jnp.zeros((LANES, 1), jnp.float32)
    counts = jnp.zeros((LANES, 1), jnp.float32)
    for side in range(2):
        member = ids == seq_ref[:, side * half : (side + 1) * half]
        sums = sums + jnp.sum(jnp.where(member, final[side, 2:3], 0.0), axis=1, keepdims=True)
        counts = counts + jnp.sum(member.astype(jnp.float32), axis=1, keepdims=True)
    means = sums / jnp.maximum(counts, 1.0)
    out_ref[...] = jnp.zeros_like(out_ref)
    out_ref[3:4, :] = jnp.transpose(jnp.broadcast_to(means, (LANES, LANES)))[0:1]
    for w in range(n):

        @pl.when(me == w)
        def _():
            start = (w % (n // 2)) * own_rows
            out_ref[0:3, 0:own_rows] = final[w // (n // 2), 0:3, start : start + own_rows]

    for k in range(1, n):
        row_copy(lax.rem(me + k, n), me).wait_send()
        pass_rows(lax.rem(me + k, n), my_part).wait_send()

    def drain(c, carry):
        @pl.when(me != last)
        def _():
            chunk_copy(0, c, up).wait_send()

        @pl.when(me != 0)
        def _():
            chunk_copy(1, c, down).wait_send()

        return carry

    lax.fori_loop(max(items - slots, 0), items, drain, 0)

    def drain_bounds(t, carry):
        @pl.when(me != last)
        def _():
            bound_copy(0, t, up).wait_send()

        @pl.when(me != 0)
        def _():
            bound_copy(1, t, down).wait_send()

        return carry

    lax.fori_loop(0, items // tile, drain_bounds, 0)

    @pl.when((me == 0) | (me == last))
    def _():
        for k in range(1, nv):
            stats_copy(lax.rem(my_vocab + k, nv), my_vocab).wait_send()
        for k in range(1, n):
            final_copy(0, lax.rem(me + k, n)).wait_send()


def tile_of(chunks):
    return max(k for k in range(1, 9) if chunks % k == 0)


def solution(mesh):
    n, nv = mesh.shape["width"], mesh.shape["vocab"]

    def local(hidden, gain, unembed, targets, seq_ids):
        own_rows, width_dim = hidden.shape
        share, columns = unembed.shape
        half = (n // 2) * own_rows
        items = GROUPS * (columns // LANES)
        tile = tile_of(columns // LANES)
        vmem = pl.BlockSpec(memory_space=pltpu.VMEM)
        out = pl.pallas_call(
            functools.partial(kernel, n, nv),
            out_shape=jax.ShapeDtypeStruct((8, LANES), jnp.float32),
            in_specs=[vmem, vmem, pl.BlockSpec(memory_space=pl.ANY), vmem, vmem],
            out_specs=vmem,
            scratch_shapes=[
                pltpu.VMEM((share, columns), jnp.bfloat16),
                pltpu.VMEM((n, own_rows, share), jnp.bfloat16),
                pltpu.VMEM((n, own_rows, share), jnp.bfloat16),
                pltpu.VMEM((2, items, half // GROUPS, LANES), jnp.int16),
                pltpu.VMEM((2, tile, half // GROUPS, LANES), jnp.float32),
                pltpu.VMEM((2, items // tile, 8, LANES), jnp.float32),
                pltpu.VMEM((2, 2, 8, LANES), jnp.float32),
                pltpu.VMEM((2, half, LANES), jnp.float32),
                pltpu.VMEM((4, half, LANES), jnp.float32),
                pltpu.VMEM((2, 8, half), jnp.float32),
                pltpu.VMEM((nv, 8, half), jnp.float32),
                pltpu.VMEM((2, 8, half), jnp.float32),
                pltpu.SemaphoreType.DMA((2,)),
                pltpu.SemaphoreType.DMA,
                pltpu.SemaphoreType.DMA((n,)),
                pltpu.SemaphoreType.DMA((n,)),
                pltpu.SemaphoreType.DMA((n,)),
                pltpu.SemaphoreType.DMA((n,)),
                pltpu.SemaphoreType.DMA((2, (n - 1) * LAG + 1)),
                pltpu.SemaphoreType.DMA((2, (n - 1) * LAG + 1)),
                pltpu.SemaphoreType.DMA((2, items // tile)),
                pltpu.SemaphoreType.DMA((2, items // tile)),
                pltpu.SemaphoreType.DMA((nv,)),
                pltpu.SemaphoreType.DMA((nv,)),
                pltpu.SemaphoreType.DMA((n,)),
                pltpu.SemaphoreType.DMA((2,)),
            ],
            compiler_params=pltpu.CompilerParams(
                collective_id=0, has_side_effects=True, vmem_limit_bytes=66_000_000
            ),
        )(hidden, gain, unembed, targets[None, :], seq_ids[None, :])
        return out[0, :own_rows], out[1, :own_rows], out[2, :own_rows], out[3, :SEQS]

    return jax.shard_map(
        local,
        mesh=mesh,
        in_specs=(P("width", None), P(), P("width", "vocab"), P(), P()),
        out_specs=(P("width"), P("width"), P("width"), P()),
        check_vma=False,
    )
```

```python
import functools

import jax
import jax.numpy as jnp
from jax import lax
from jax.experimental import pallas as pl
from jax.experimental.pallas import tpu as pltpu
from jax.sharding import PartitionSpec as P

SEQS = 48
LANES = 128
LAG = 9
GROUPS = 2
PAIR_FROM = 2
PART_ROWS = 8
LOWEST = -1e38
LEVELS = 32760.0
TINY = 1e-30
MESH = pl.DeviceIdType.MESH


def kernel(
    n, nv, hidden_ref, gain_ref, unembed_ref, targets_ref, seq_ref, out_ref,
    weights, blocks, rows_in, buf, part, peaks, bound, steps, target_cols, state, packed, gathered,
    w_sem, own_sem, x_send, x_recv, p_send, p_recv, c_send, c_recv, b_send, b_recv,
    v_send, v_recv,
):
    me = lax.axis_index("width")
    my_vocab = lax.axis_index("vocab")
    own_rows, width_dim = hidden_ref.shape
    share = width_dim // n
    half = (n // 2) * own_rows
    chunks = unembed_ref.shape[1] // LANES
    last = n - 1
    group_blocks = n // 2 // GROUPS
    group_rows = group_blocks * own_rows
    items = GROUPS * chunks
    slots = last * LAG + 1
    tile = tile_of(chunks)
    tiles = chunks // tile

    early = tile * LANES
    loads = []
    for k, cols in enumerate((pl.ds(0, early), pl.ds(early, chunks * LANES - early))):
        loads.append(
            pltpu.make_async_copy(unembed_ref.at[:, cols], weights.at[:, cols], w_sem.at[k])
        )
        loads[k].start()

    barrier = pltpu.get_barrier_semaphore()
    for k in range(1, n):
        pl.semaphore_signal(
            barrier, inc=1, device_id={"width": lax.rem(me + k, n)}, device_id_type=MESH
        )
    for k in range(1, nv):
        pl.semaphore_signal(
            barrier, inc=1, device_id={"vocab": lax.rem(my_vocab + k, nv)}, device_id_type=MESH
        )

    values = hidden_ref[...].astype(jnp.float32)
    square = jnp.mean(values * values, axis=1, keepdims=True)
    normed = (values * lax.rsqrt(square + 1e-05) * gain_ref[...][None, :]).astype(jnp.bfloat16)
    for j in range(n):
        blocks[j] = normed[:, j * share : (j + 1) * share]

    pl.semaphore_wait(barrier, n - 1 + nv - 1)

    parts = parts_of(nv, own_rows)
    part_rows = own_rows // parts
    place = lax.rem(my_vocab, parts)

    def part_of(k):
        return pl.ds(pl.multiple_of(k * part_rows, part_rows), part_rows)

    def row_copy(peer, source):
        return pltpu.make_async_remote_copy(
            src_ref=blocks.at[peer, part_of(place)],
            dst_ref=rows_in.at[source, part_of(place)],
            send_sem=x_send.at[peer],
            recv_sem=x_recv.at[source],
            device_id={"width": peer},
            device_id_type=MESH,
        )

    def pass_rows(source, peer, owner):
        return pltpu.make_async_remote_copy(
            src_ref=rows_in.at[source, part_of(owner)],
            dst_ref=rows_in.at[source, part_of(owner)],
            send_sem=p_send.at[source * parts + peer],
            recv_sem=p_recv.at[source * parts + owner],
            device_id={"vocab": my_vocab - place + peer},
            device_id_type=MESH,
        )

    half_rows = own_rows // 2
    parity = lax.rem(place, 2)
    partner = place + 1 - 2 * parity

    def half_of(k):
        return pl.ds(pl.multiple_of(k * half_rows, half_rows), half_rows)

    def near_copy(peer, source):
        return pltpu.make_async_remote_copy(
            src_ref=blocks.at[peer, half_of(parity)],
            dst_ref=rows_in.at[source, half_of(parity)],
            send_sem=x_send.at[peer],
            recv_sem=x_recv.at[source],
            device_id={"width": peer},
            device_id_type=MESH,
        )

    def near_pass(source, half_index, owner):
        return pltpu.make_async_remote_copy(
            src_ref=rows_in.at[source, half_of(half_index)],
            dst_ref=rows_in.at[source, half_of(half_index)],
            send_sem=p_send.at[source * parts + partner],
            recv_sem=p_recv.at[source * parts + owner],
            device_id={"vocab": my_vocab - place + partner},
            device_id_type=MESH,
        )

    at_end = (me == 0) | (me == last)

    def peer_of(k):
        return lax.rem(me + jnp.where(me < n // 2, k, n - k), n)

    def is_near(source):
        return ((source == 0) & (me == 1)) | ((source == last) & (me == last - 1))

    @pl.when(at_end)
    def _():
        near_copy(peer_of(1), me).start()

    @pl.when(jnp.logical_not(at_end))
    def _():
        row_copy(peer_of(1), me).start()

    for k in range(2, n):
        row_copy(peer_of(k), me).start()

    own = pltpu.make_async_copy(blocks.at[me], rows_in.at[me], own_sem)
    own.start()

    target_row = targets_ref[...].astype(jnp.float32)
    target_all = jnp.transpose(jnp.broadcast_to(target_row, (LANES, 2 * half)))
    target_cols[0] = target_all[:half]
    target_cols[1] = target_all[half:]
    state[0] = jnp.full((half, LANES), LOWEST, jnp.float32)
    for k in range(1, 4):
        state[k] = jnp.zeros((half, LANES), jnp.float32)

    own.wait()
    loads[0].wait()

    def chunk_copy(side, c, peer):
        return pltpu.make_async_remote_copy(
            src_ref=buf.at[side, c],
            dst_ref=buf.at[side, c],
            send_sem=c_send.at[side, lax.rem(c, slots)],
            recv_sem=c_recv.at[side, lax.rem(c, slots)],
            device_id={"width": peer},
            device_id_type=MESH,
        )

    first_col = my_vocab * (chunks * LANES)
    lane = lax.broadcasted_iota(jnp.int32, (half, LANES), 1)
    item_lane = lax.broadcasted_iota(jnp.int32, (group_rows, LANES), 1)

    def bound_copy(side, t, peer):
        return pltpu.make_async_remote_copy(
            src_ref=bound.at[side, t],
            dst_ref=bound.at[side, t],
            send_sem=b_send.at[side, t],
            recv_sem=b_recv.at[side, t],
            device_id={"width": peer},
            device_id_type=MESH,
        )

    def by_vreg(values):
        return values.reshape(group_rows // 8, 8, LANES)

    def keep(side, group, c, t, logits):
        peak = jnp.full((8, LANES), TINY, jnp.float32)
        for j in range(tile):
            piece = logits[:, j * LANES : (j + 1) * LANES]
            part[side, group * chunks + c + j] = piece
            peak = jnp.maximum(peak, jnp.max(jnp.abs(by_vreg(piece)), axis=0))
        peaks[side, t] = peak

    def tile_logits(x, c):
        cols = pl.ds(pl.multiple_of(c * LANES, LANES), tile * LANES)
        x = x.reshape(x.shape[0] * own_rows, share)
        return jnp.dot(x, weights[:, cols], preferred_element_type=jnp.float32)

    def open_tile(side, group, first_block, c, t, head, tail, peer):
        for g in range(GROUPS):
            start = g * group_blocks if side == 0 else n - (g + 1) * group_blocks

            @pl.when(t == g)
            def _():
                for w in range(start, start + group_blocks):
                    if w in (0, last):

                        @pl.when(is_near(w))
                        def _():
                            near_copy(w, w).wait_recv()
                            near_pass(w, parity, place).start()

                    @pl.when((me != w) & jnp.logical_not(is_near(w)))
                    def _():
                        row_copy(w, w).wait_recv()
                        for k in range(1, parts):
                            pass_rows(w, lax.rem(place + k, parts), place).start()

            @pl.when(t == g * PAIR_FROM)
            def _():
                for w in range(start, start + group_blocks):
                    if w in (0, last):

                        @pl.when(is_near(w))
                        def _():
                            near_pass(w, 1 - parity, partner).wait_recv()

                    @pl.when((me != w) & jnp.logical_not(is_near(w)))
                    def _():
                        for k in range(1, parts):
                            other = lax.rem(place + k, parts)
                            pass_rows(w, other, other).wait_recv()

        @pl.when(t - group * tiles < PAIR_FROM)
        def _():
            keep(side, group, c, t, tile_logits(rows_in[pl.ds(first_block, group_blocks)], c))

        @pl.when((group == 0) & (t >= PAIR_FROM))
        def _():
            logits = tile_logits(rows_in[side * (n // 2) : (side + 1) * (n // 2)], c)
            for g in range(GROUPS):
                start = (g if side == 0 else GROUPS - 1 - g) * group_rows
                keep(side, g, c, t + g * tiles, logits[start : start + group_rows])

        def announce(limit):
            bound[side, t] = limit
            steps[side, 1] = LEVELS / limit
            bound_copy(side, t, peer).start()

        @pl.when(me == head)
        def _():
            announce(peaks[side, t])

        @pl.when(me != head)
        def _():
            bound_copy(side, t, peer).wait_recv()
            incoming = bound[side, t]
            steps[side, 0] = incoming * (1.0 / LEVELS)

            @pl.when(me != tail)
            def _():
                announce(incoming + peaks[side, t])

    def to_codes(side, values):
        scaled = by_vreg(values) * steps[side, 1][None]
        return jnp.round(scaled).astype(jnp.int32).astype(jnp.int16).reshape(group_rows, LANES)

    def from_codes(side, codes):
        values = by_vreg(codes.astype(jnp.int32).astype(jnp.float32)) * steps[side, 0][None]
        return values.reshape(group_rows, LANES)

    def take_stats(side, first_block, c, logits):
        rows = pl.ds(pl.multiple_of((first_block - side * (n // 2)) * own_rows, 8), group_rows)
        column = (first_col + c * LANES + item_lane).astype(jnp.float32)
        old_max = state[0, rows]
        new_max = jnp.maximum(old_max, logits)
        scale = jnp.exp(old_max - new_max)
        shifted = jnp.exp(logits - new_max)
        state[0, rows] = new_max
        state[1, rows] = state[1, rows] * scale + shifted
        state[2, rows] = state[2, rows] * scale + shifted * logits
        state[3, rows] = state[3, rows] + jnp.where(column == target_cols[side, rows], logits, 0.0)

    def advance(side, item, head, tail, peer):
        @pl.when((item >= 0) & (item < items))
        def _():
            group = item // chunks
            c = item - group * chunks
            first_block = group * group_blocks if side == 0 else n - (group + 1) * group_blocks
            @pl.when(lax.rem(item, tile) == 0)
            def _():
                open_tile(side, group, first_block, c, item // tile, head, tail, peer)

            @pl.when((me != tail) & (item >= slots))
            def _():
                chunk_copy(side, item - slots, peer).wait_send()

            @pl.when(me == head)
            def _():
                buf[side, item] = to_codes(side, part[side, item])
                chunk_copy(side, item, peer).start()

            @pl.when(me != head)
            def _():
                chunk_copy(side, item, peer).wait_recv()
                total = from_codes(side, buf[side, item]) + part[side, item]

                @pl.when(me != tail)
                def _():
                    buf[side, item] = to_codes(side, total)
                    chunk_copy(side, item, peer).start()

                @pl.when(me == tail)
                def _():
                    take_stats(side, first_block, c, total)

    down = lax.rem(me + n - 1, n)
    up = lax.rem(me + 1, n)

    def step(s, carry):
        @pl.when(s == 1)
        def _():
            loads[1].wait()

        advance(0, s - me * LAG, 0, last, up)
        advance(1, s - (last - me) * LAG, last, 0, down)
        return carry

    lax.fori_loop(0, items + last * LAG, step, 0)

    def stats_copy(side, w, v, source):
        return pltpu.make_async_remote_copy(
            src_ref=packed,
            dst_ref=gathered.at[side, source],
            send_sem=v_send.at[w * nv + v],
            recv_sem=v_recv.at[side * nv + source],
            device_id={"width": w, "vocab": v},
            device_id_type=MESH,
        )

    def for_others(side, act):
        def body(i, carry):
            far = i // nv
            w = far if side == 0 else last - far
            v = lax.rem(my_vocab + lax.rem(i, nv), nv)
            act(stats_copy(side, w, v, my_vocab))
            return carry

        lax.fori_loop(0, last * nv, body, 0)
        for k in range(1, nv):
            act(stats_copy(side, last if side == 0 else 0, lax.rem(my_vocab + k, nv), my_vocab))

    def finish(side):
        lane_max = state[0]
        row_max = jnp.max(lane_max, axis=1, keepdims=True)
        scale = jnp.exp(lane_max - row_max)
        columns = (
            row_max,
            jnp.sum(state[1] * scale, axis=1, keepdims=True),
            jnp.sum(state[2] * scale, axis=1, keepdims=True),
            jnp.sum(state[3], axis=1, keepdims=True),
        )
        wide = jnp.zeros((half, LANES), jnp.float32)
        for k in range(4):
            wide = jnp.where(lane == k, columns[k], wide)
        flat = jnp.transpose(wide)[:4]
        packed[...] = flat
        for_others(side, lambda copy: copy.start())
        gathered[side, my_vocab] = flat

    @pl.when(me == last)
    def _():
        finish(0)

    @pl.when(me == 0)
    def _():
        finish(1)

    def results(side):
        @pl.when(me != (last if side == 0 else 0))
        def _():
            stats_copy(side, me, my_vocab, my_vocab).wait_recv()

        for k in range(1, nv):
            stats_copy(side, me, my_vocab, lax.rem(my_vocab + k, nv)).wait_recv()

        pieces = [gathered[side, v] for v in range(nv)]
        top = functools.reduce(jnp.maximum, [piece[0:1] for piece in pieces])
        total = jnp.zeros_like(top)
        weighted = jnp.zeros_like(top)
        target = jnp.zeros_like(top)
        for piece in pieces:
            factor = jnp.exp(piece[0:1] - top)
            total = total + piece[1:2] * factor
            weighted = weighted + piece[2:3] * factor
            target = target + piece[3:4]
        log_normalizer = top + jnp.log(total)
        return log_normalizer, log_normalizer - weighted / total, target - log_normalizer

    final = [results(0), results(1)]

    ids = lax.broadcasted_iota(jnp.int32, (LANES, half), 0)
    sums = jnp.zeros((LANES, 1), jnp.float32)
    counts = jnp.zeros((LANES, 1), jnp.float32)
    for side in range(2):
        in_sequence = ids == seq_ref[:, side * half : (side + 1) * half]
        sums = sums + jnp.sum(jnp.where(in_sequence, final[side][2], 0.0), axis=1, keepdims=True)
        counts = counts + jnp.sum(in_sequence.astype(jnp.float32), axis=1, keepdims=True)
    means = sums / jnp.maximum(counts, 1.0)
    out_ref[...] = jnp.zeros_like(out_ref)
    out_ref[3:4, :] = jnp.transpose(jnp.broadcast_to(means, (LANES, LANES)))[0:1]
    for w in range(n):

        @pl.when(me == w)
        def _():
            start = (w % (n // 2)) * own_rows
            for k in range(3):
                mine = final[w // (n // 2)][k][:, start : start + own_rows]
                out_ref[k : k + 1, 0:own_rows] = mine

    @pl.when(at_end)
    def _():
        near_copy(peer_of(1), me).wait_send()

    @pl.when(jnp.logical_not(at_end))
    def _():
        row_copy(peer_of(1), me).wait_send()

    for k in range(2, n):
        row_copy(peer_of(k), me).wait_send()

    for k in range(1, n):
        source = lax.rem(me + k, n)

        @pl.when(is_near(source))
        def _():
            near_pass(source, parity, place).wait_send()

        @pl.when(jnp.logical_not(is_near(source)))
        def _():
            for j in range(1, parts):
                pass_rows(source, lax.rem(place + j, parts), place).wait_send()

    def drain(c, carry):
        @pl.when(me != last)
        def _():
            chunk_copy(0, c, up).wait_send()

        @pl.when(me != 0)
        def _():
            chunk_copy(1, c, down).wait_send()

        return carry

    lax.fori_loop(max(items - slots, 0), items, drain, 0)

    def drain_bounds(t, carry):
        @pl.when(me != last)
        def _():
            bound_copy(0, t, up).wait_send()

        @pl.when(me != 0)
        def _():
            bound_copy(1, t, down).wait_send()

        return carry

    lax.fori_loop(0, items // tile, drain_bounds, 0)

    @pl.when(me == last)
    def _():
        for_others(0, lambda copy: copy.wait_send())

    @pl.when(me == 0)
    def _():
        for_others(1, lambda copy: copy.wait_send())


def split_outputs(packed_ref, *refs):
    for k, ref in enumerate(refs):
        ref[...] = packed_ref[k : k + 1, : ref.shape[1]]


def tile_of(chunks):
    return max(k for k in range(1, 9) if chunks % k == 0)


def parts_of(nv, own_rows):
    return min(nv, own_rows // PART_ROWS)


def solution(mesh):
    n, nv = mesh.shape["width"], mesh.shape["vocab"]

    def local(hidden, gain, unembed, targets, seq_ids):
        own_rows, width_dim = hidden.shape
        share, columns = unembed.shape
        half = (n // 2) * own_rows
        items = GROUPS * (columns // LANES)
        tile = tile_of(columns // LANES)
        vmem = pl.BlockSpec(memory_space=pltpu.VMEM)
        out = pl.pallas_call(
            functools.partial(kernel, n, nv),
            out_shape=jax.ShapeDtypeStruct((8, LANES), jnp.float32),
            in_specs=[vmem, vmem, pl.BlockSpec(memory_space=pl.ANY), vmem, vmem],
            out_specs=vmem,
            scratch_shapes=[
                pltpu.VMEM((share, columns), jnp.bfloat16),
                pltpu.VMEM((n, own_rows, share), jnp.bfloat16),
                pltpu.VMEM((n, own_rows, share), jnp.bfloat16),
                pltpu.VMEM((2, items, half // GROUPS, LANES), jnp.int16),
                pltpu.VMEM((2, items, half // GROUPS, LANES), jnp.float32),
                pltpu.VMEM((2, items // tile, 8, LANES), jnp.float32),
                pltpu.VMEM((2, items // tile, 8, LANES), jnp.float32),
                pltpu.VMEM((2, 2, 8, LANES), jnp.float32),
                pltpu.VMEM((2, half, LANES), jnp.float32),
                pltpu.VMEM((4, half, LANES), jnp.float32),
                pltpu.VMEM((4, half), jnp.float32),
                pltpu.VMEM((2, nv, 4, half), jnp.float32),
                pltpu.SemaphoreType.DMA((2,)),
                pltpu.SemaphoreType.DMA,
                pltpu.SemaphoreType.DMA((n,)),
                pltpu.SemaphoreType.DMA((n,)),
                pltpu.SemaphoreType.DMA((n * parts_of(nv, own_rows),)),
                pltpu.SemaphoreType.DMA((n * parts_of(nv, own_rows),)),
                pltpu.SemaphoreType.DMA((2, (n - 1) * LAG + 1)),
                pltpu.SemaphoreType.DMA((2, (n - 1) * LAG + 1)),
                pltpu.SemaphoreType.DMA((2, items // tile)),
                pltpu.SemaphoreType.DMA((2, items // tile)),
                pltpu.SemaphoreType.DMA((n * nv,)),
                pltpu.SemaphoreType.DMA((2 * nv,)),
            ],
            compiler_params=pltpu.CompilerParams(
                collective_id=0, has_side_effects=True, vmem_limit_bytes=66_000_000
            ),
        )(hidden, gain, unembed, targets[None, :], seq_ids[None, :])
        split = pl.pallas_call(
            split_outputs,
            out_shape=[jax.ShapeDtypeStruct((1, k), jnp.float32) for k in 3 * [own_rows] + [SEQS]],
            in_specs=[vmem],
            out_specs=[vmem] * 4,
        )(out)
        return tuple(array[0] for array in split)

    return jax.shard_map(
        local,
        mesh=mesh,
        in_specs=(P("width", None), P(), P("width", "vocab"), P(), P()),
        out_specs=(P("width"), P("width"), P("width"), P()),
        check_vma=False,
    )
```

```python
import functools

import jax
import jax.numpy as jnp
from jax import lax
from jax.experimental import pallas as pl
from jax.experimental.pallas import tpu as pltpu
from jax.sharding import PartitionSpec as P

SEQS = 48
LANES = 128
LAG = 9
GROUPS = 2
PAIR_FROM = 2
PART_ROWS = 8
LOWEST = -1e38
LEVELS = 32760.0
TINY = 1e-30
MESH = pl.DeviceIdType.MESH


def kernel(
    n, nv, hidden_ref, gain_ref, unembed_ref, targets_ref, seq_ref, out_ref,
    weights, blocks, rows_in, buf, part, peaks, bound, steps, target_cols, state, packed, gathered,
    w_sem, own_sem, x_send, x_recv, p_send, p_recv, c_send, c_recv, b_send, b_recv,
    v_send, v_recv,
):
    me = lax.axis_index("width")
    my_vocab = lax.axis_index("vocab")
    own_rows, width_dim = hidden_ref.shape
    share = width_dim // n
    half = (n // 2) * own_rows
    chunks = unembed_ref.shape[1] // LANES
    last = n - 1
    group_blocks = n // 2 // GROUPS
    group_rows = group_blocks * own_rows
    items = GROUPS * chunks
    slots = last * LAG + 1
    tile = tile_of(chunks)
    tiles = chunks // tile

    early = tile * LANES
    loads = []
    for k, cols in enumerate((pl.ds(0, early), pl.ds(early, chunks * LANES - early))):
        loads.append(
            pltpu.make_async_copy(unembed_ref.at[:, cols], weights.at[:, cols], w_sem.at[k])
        )
        loads[k].start()

    barrier = pltpu.get_barrier_semaphore()
    for k in range(1, n):
        pl.semaphore_signal(
            barrier, inc=1, device_id={"width": lax.rem(me + k, n)}, device_id_type=MESH
        )
    for k in range(1, nv):
        pl.semaphore_signal(
            barrier, inc=1, device_id={"vocab": lax.rem(my_vocab + k, nv)}, device_id_type=MESH
        )

    values = hidden_ref[...].astype(jnp.float32)
    square = jnp.mean(values * values, axis=1, keepdims=True)
    normed = (values * lax.rsqrt(square + 1e-05) * gain_ref[...][None, :]).astype(jnp.bfloat16)
    for j in range(n):
        blocks[j] = normed[:, j * share : (j + 1) * share]

    pl.semaphore_wait(barrier, n - 1 + nv - 1)

    parts = parts_of(nv, own_rows)
    part_rows = own_rows // parts
    place = lax.rem(my_vocab, parts)

    def part_of(k):
        return pl.ds(pl.multiple_of(k * part_rows, part_rows), part_rows)

    def row_copy(peer, source):
        return pltpu.make_async_remote_copy(
            src_ref=blocks.at[peer, part_of(place)],
            dst_ref=rows_in.at[source, part_of(place)],
            send_sem=x_send.at[peer],
            recv_sem=x_recv.at[source],
            device_id={"width": peer},
            device_id_type=MESH,
        )

    def pass_rows(source, peer, owner):
        return pltpu.make_async_remote_copy(
            src_ref=rows_in.at[source, part_of(owner)],
            dst_ref=rows_in.at[source, part_of(owner)],
            send_sem=p_send.at[source * parts + peer],
            recv_sem=p_recv.at[source * parts + owner],
            device_id={"vocab": my_vocab - place + peer},
            device_id_type=MESH,
        )

    half_rows = own_rows // 2
    parity = lax.rem(place, 2)
    partner = place + 1 - 2 * parity

    def half_of(k):
        return pl.ds(pl.multiple_of(k * half_rows, half_rows), half_rows)

    def near_copy(peer, source):
        return pltpu.make_async_remote_copy(
            src_ref=blocks.at[peer, half_of(parity)],
            dst_ref=rows_in.at[source, half_of(parity)],
            send_sem=x_send.at[peer],
            recv_sem=x_recv.at[source],
            device_id={"width": peer},
            device_id_type=MESH,
        )

    def near_pass(source, half_index, owner):
        return pltpu.make_async_remote_copy(
            src_ref=rows_in.at[source, half_of(half_index)],
            dst_ref=rows_in.at[source, half_of(half_index)],
            send_sem=p_send.at[source * parts + partner],
            recv_sem=p_recv.at[source * parts + owner],
            device_id={"vocab": my_vocab - place + partner},
            device_id_type=MESH,
        )

    at_end = (me == 0) | (me == last)

    def peer_of(k):
        return lax.rem(me + jnp.where(me < n // 2, k, n - k), n)

    def is_near(source):
        return ((source == 0) & (me == 1)) | ((source == last) & (me == last - 1))

    @pl.when(at_end)
    def _():
        near_copy(peer_of(1), me).start()

    @pl.when(jnp.logical_not(at_end))
    def _():
        row_copy(peer_of(1), me).start()

    for k in range(2, n):
        row_copy(peer_of(k), me).start()

    own = pltpu.make_async_copy(blocks.at[me], rows_in.at[me], own_sem)
    own.start()

    target_row = targets_ref[...].astype(jnp.float32)
    target_all = jnp.transpose(jnp.broadcast_to(target_row, (LANES, 2 * half)))
    target_cols[0] = target_all[:half]
    target_cols[1] = target_all[half:]
    state[0] = jnp.full((half, LANES), LOWEST, jnp.float32)
    for k in range(1, 4):
        state[k] = jnp.zeros((half, LANES), jnp.float32)

    own.wait()
    loads[0].wait()

    def chunk_copy(side, c, peer):
        return pltpu.make_async_remote_copy(
            src_ref=buf.at[side, c],
            dst_ref=buf.at[side, c],
            send_sem=c_send.at[side, lax.rem(c, slots)],
            recv_sem=c_recv.at[side, lax.rem(c, slots)],
            device_id={"width": peer},
            device_id_type=MESH,
        )

    first_col = my_vocab * (chunks * LANES)
    lane = lax.broadcasted_iota(jnp.int32, (half, LANES), 1)
    item_lane = lax.broadcasted_iota(jnp.int32, (group_rows, LANES), 1)

    def bound_copy(side, t, peer):
        return pltpu.make_async_remote_copy(
            src_ref=bound.at[side, t],
            dst_ref=bound.at[side, t],
            send_sem=b_send.at[side, t],
            recv_sem=b_recv.at[side, t],
            device_id={"width": peer},
            device_id_type=MESH,
        )

    def by_vreg(values):
        return values.reshape(group_rows // 8, 8, LANES)

    def keep(side, group, c, t, logits):
        peak = jnp.full((8, LANES), TINY, jnp.float32)
        for j in range(tile):
            piece = logits[:, j * LANES : (j + 1) * LANES]
            part[side, group * chunks + c + j] = piece
            peak = jnp.maximum(peak, jnp.max(jnp.abs(by_vreg(piece)), axis=0))
        peaks[side, t] = peak

    def tile_logits(x, c):
        cols = pl.ds(pl.multiple_of(c * LANES, LANES), tile * LANES)
        x = x.reshape(x.shape[0] * own_rows, share)
        return jnp.dot(x, weights[:, cols], preferred_element_type=jnp.float32)

    def open_tile(side, group, first_block, c, t, head, tail, peer):
        for g in range(GROUPS):
            start = g * group_blocks if side == 0 else n - (g + 1) * group_blocks

            @pl.when(t == g * PAIR_FROM)
            def _():
                for w in range(start, start + group_blocks):
                    if w in (0, last):

                        @pl.when(is_near(w))
                        def _():
                            near_pass(w, 1 - parity, partner).wait_recv()

                    @pl.when((me != w) & jnp.logical_not(is_near(w)))
                    def _():
                        for k in range(1, parts):
                            other = lax.rem(place + k, parts)
                            pass_rows(w, other, other).wait_recv()

        @pl.when(t - group * tiles < PAIR_FROM)
        def _():
            keep(side, group, c, t, tile_logits(rows_in[pl.ds(first_block, group_blocks)], c))

        @pl.when((group == 0) & (t >= PAIR_FROM))
        def _():
            logits = tile_logits(rows_in[side * (n // 2) : (side + 1) * (n // 2)], c)
            for g in range(GROUPS):
                start = (g if side == 0 else GROUPS - 1 - g) * group_rows
                keep(side, g, c, t + g * tiles, logits[start : start + group_rows])

        def announce(limit):
            bound[side, t] = limit
            steps[side, 1] = LEVELS / limit
            bound_copy(side, t, peer).start()

        @pl.when(me == head)
        def _():
            announce(peaks[side, t])

        @pl.when(me != head)
        def _():
            bound_copy(side, t, peer).wait_recv()
            incoming = bound[side, t]
            steps[side, 0] = incoming * (1.0 / LEVELS)

            @pl.when(me != tail)
            def _():
                announce(incoming + peaks[side, t])

    def to_codes(side, values):
        scaled = by_vreg(values) * steps[side, 1][None]
        return jnp.round(scaled).astype(jnp.int32).astype(jnp.int16).reshape(group_rows, LANES)

    def from_codes(side, codes):
        values = by_vreg(codes.astype(jnp.int32).astype(jnp.float32)) * steps[side, 0][None]
        return values.reshape(group_rows, LANES)

    def take_stats(side, first_block, c, logits):
        rows = pl.ds(pl.multiple_of((first_block - side * (n // 2)) * own_rows, 8), group_rows)
        column = (first_col + c * LANES + item_lane).astype(jnp.float32)
        old_max = state[0, rows]
        new_max = jnp.maximum(old_max, logits)
        scale = jnp.exp(old_max - new_max)
        shifted = jnp.exp(logits - new_max)
        state[0, rows] = new_max
        state[1, rows] = state[1, rows] * scale + shifted
        state[2, rows] = state[2, rows] * scale + shifted * logits
        state[3, rows] = state[3, rows] + jnp.where(column == target_cols[side, rows], logits, 0.0)

    def advance(side, item, head, tail, peer):
        @pl.when((item >= 0) & (item < items))
        def _():
            group = item // chunks
            c = item - group * chunks
            first_block = group * group_blocks if side == 0 else n - (group + 1) * group_blocks
            @pl.when(lax.rem(item, tile) == 0)
            def _():
                open_tile(side, group, first_block, c, item // tile, head, tail, peer)

            @pl.when((me != tail) & (item >= slots))
            def _():
                chunk_copy(side, item - slots, peer).wait_send()

            @pl.when(me == head)
            def _():
                buf[side, item] = to_codes(side, part[side, item])
                chunk_copy(side, item, peer).start()

            @pl.when(me != head)
            def _():
                chunk_copy(side, item, peer).wait_recv()
                total = from_codes(side, buf[side, item]) + part[side, item]

                @pl.when(me != tail)
                def _():
                    buf[side, item] = to_codes(side, total)
                    chunk_copy(side, item, peer).start()

                @pl.when(me == tail)
                def _():
                    take_stats(side, first_block, c, total)

    down = lax.rem(me + n - 1, n)
    up = lax.rem(me + 1, n)

    def take_near(w):
        @pl.when(is_near(w))
        def _():
            near_copy(w, w).wait_recv()
            near_pass(w, parity, place).start()

    def take_rows(sources, here):
        for w in sources:

            @pl.when(here & (me != w) & jnp.logical_not(is_near(w)))
            def _():
                row_copy(w, w).wait_recv()
                for k in range(1, parts):
                    pass_rows(w, lax.rem(place + k, parts), place).start()

    take_near(0)
    take_near(last)
    take_rows([*range(1, last), 0, last], jnp.logical_not(at_end))

    def step(s, carry):
        @pl.when((s == tile) & at_end)
        def _():
            take_rows(range(1, n // 2), me == 0)
            take_rows(range(n // 2, last), me == last)

        @pl.when((s == 2 * tile) & at_end)
        def _():
            take_rows(range(n // 2, n), me == 0)
            take_rows(range(n // 2), me == last)

        @pl.when(s == 1)
        def _():
            loads[1].wait()

        advance(0, s - me * LAG, 0, last, up)
        advance(1, s - (last - me) * LAG, last, 0, down)
        return carry

    lax.fori_loop(0, items + last * LAG, step, 0)

    def stats_copy(side, w, v, source):
        return pltpu.make_async_remote_copy(
            src_ref=packed,
            dst_ref=gathered.at[side, source],
            send_sem=v_send.at[w * nv + v],
            recv_sem=v_recv.at[side * nv + source],
            device_id={"width": w, "vocab": v},
            device_id_type=MESH,
        )

    def for_others(side, act):
        def body(i, carry):
            far = i // nv
            w = far if side == 0 else last - far
            v = lax.rem(my_vocab + lax.rem(i, nv), nv)
            act(stats_copy(side, w, v, my_vocab))
            return carry

        lax.fori_loop(0, last * nv, body, 0)
        for k in range(1, nv):
            act(stats_copy(side, last if side == 0 else 0, lax.rem(my_vocab + k, nv), my_vocab))

    def finish(side):
        lane_max = state[0]
        row_max = jnp.max(lane_max, axis=1, keepdims=True)
        scale = jnp.exp(lane_max - row_max)
        columns = (
            row_max,
            jnp.sum(state[1] * scale, axis=1, keepdims=True),
            jnp.sum(state[2] * scale, axis=1, keepdims=True),
            jnp.sum(state[3], axis=1, keepdims=True),
        )
        wide = jnp.zeros((half, LANES), jnp.float32)
        for k in range(4):
            wide = jnp.where(lane == k, columns[k], wide)
        flat = jnp.transpose(wide)[:4]
        packed[...] = flat
        for_others(side, lambda copy: copy.start())
        gathered[side, my_vocab] = flat

    @pl.when(me == last)
    def _():
        finish(0)

    @pl.when(me == 0)
    def _():
        finish(1)

    def results(side):
        @pl.when(me != (last if side == 0 else 0))
        def _():
            stats_copy(side, me, my_vocab, my_vocab).wait_recv()

        for k in range(1, nv):
            stats_copy(side, me, my_vocab, lax.rem(my_vocab + k, nv)).wait_recv()

        pieces = [gathered[side, v] for v in range(nv)]
        top = functools.reduce(jnp.maximum, [piece[0:1] for piece in pieces])
        total = jnp.zeros_like(top)
        weighted = jnp.zeros_like(top)
        target = jnp.zeros_like(top)
        for piece in pieces:
            factor = jnp.exp(piece[0:1] - top)
            total = total + piece[1:2] * factor
            weighted = weighted + piece[2:3] * factor
            target = target + piece[3:4]
        log_normalizer = top + jnp.log(total)
        return log_normalizer, log_normalizer - weighted / total, target - log_normalizer

    final = [results(0), results(1)]

    ids = lax.broadcasted_iota(jnp.int32, (LANES, half), 0)
    sums = jnp.zeros((LANES, 1), jnp.float32)
    counts = jnp.zeros((LANES, 1), jnp.float32)
    for side in range(2):
        in_sequence = ids == seq_ref[:, side * half : (side + 1) * half]
        sums = sums + jnp.sum(jnp.where(in_sequence, final[side][2], 0.0), axis=1, keepdims=True)
        counts = counts + jnp.sum(in_sequence.astype(jnp.float32), axis=1, keepdims=True)
    means = sums / jnp.maximum(counts, 1.0)
    out_ref[...] = jnp.zeros_like(out_ref)
    out_ref[3:4, :] = jnp.transpose(jnp.broadcast_to(means, (LANES, LANES)))[0:1]
    for w in range(n):

        @pl.when(me == w)
        def _():
            start = (w % (n // 2)) * own_rows
            for k in range(3):
                mine = final[w // (n // 2)][k][:, start : start + own_rows]
                out_ref[k : k + 1, 0:own_rows] = mine

    @pl.when(at_end)
    def _():
        near_copy(peer_of(1), me).wait_send()

    @pl.when(jnp.logical_not(at_end))
    def _():
        row_copy(peer_of(1), me).wait_send()

    for k in range(2, n):
        row_copy(peer_of(k), me).wait_send()

    for k in range(1, n):
        source = lax.rem(me + k, n)

        @pl.when(is_near(source))
        def _():
            near_pass(source, parity, place).wait_send()

        @pl.when(jnp.logical_not(is_near(source)))
        def _():
            for j in range(1, parts):
                pass_rows(source, lax.rem(place + j, parts), place).wait_send()

    def drain(c, carry):
        @pl.when(me != last)
        def _():
            chunk_copy(0, c, up).wait_send()

        @pl.when(me != 0)
        def _():
            chunk_copy(1, c, down).wait_send()

        return carry

    lax.fori_loop(max(items - slots, 0), items, drain, 0)

    def drain_bounds(t, carry):
        @pl.when(me != last)
        def _():
            bound_copy(0, t, up).wait_send()

        @pl.when(me != 0)
        def _():
            bound_copy(1, t, down).wait_send()

        return carry

    lax.fori_loop(0, items // tile, drain_bounds, 0)

    @pl.when(me == last)
    def _():
        for_others(0, lambda copy: copy.wait_send())

    @pl.when(me == 0)
    def _():
        for_others(1, lambda copy: copy.wait_send())


def split_outputs(packed_ref, *refs):
    for k, ref in enumerate(refs):
        ref[...] = packed_ref[k : k + 1, : ref.shape[1]]


def tile_of(chunks):
    return max(k for k in range(1, 9) if chunks % k == 0)


def parts_of(nv, own_rows):
    return min(nv, own_rows // PART_ROWS)


def solution(mesh):
    n, nv = mesh.shape["width"], mesh.shape["vocab"]

    def local(hidden, gain, unembed, targets, seq_ids):
        own_rows, width_dim = hidden.shape
        share, columns = unembed.shape
        half = (n // 2) * own_rows
        items = GROUPS * (columns // LANES)
        tile = tile_of(columns // LANES)
        vmem = pl.BlockSpec(memory_space=pltpu.VMEM)
        out = pl.pallas_call(
            functools.partial(kernel, n, nv),
            out_shape=jax.ShapeDtypeStruct((8, LANES), jnp.float32),
            in_specs=[vmem, vmem, pl.BlockSpec(memory_space=pl.ANY), vmem, vmem],
            out_specs=vmem,
            scratch_shapes=[
                pltpu.VMEM((share, columns), jnp.bfloat16),
                pltpu.VMEM((n, own_rows, share), jnp.bfloat16),
                pltpu.VMEM((n, own_rows, share), jnp.bfloat16),
                pltpu.VMEM((2, items, half // GROUPS, LANES), jnp.int16),
                pltpu.VMEM((2, items, half // GROUPS, LANES), jnp.float32),
                pltpu.VMEM((2, items // tile, 8, LANES), jnp.float32),
                pltpu.VMEM((2, items // tile, 8, LANES), jnp.float32),
                pltpu.VMEM((2, 2, 8, LANES), jnp.float32),
                pltpu.VMEM((2, half, LANES), jnp.float32),
                pltpu.VMEM((4, half, LANES), jnp.float32),
                pltpu.VMEM((4, half), jnp.float32),
                pltpu.VMEM((2, nv, 4, half), jnp.float32),
                pltpu.SemaphoreType.DMA((2,)),
                pltpu.SemaphoreType.DMA,
                pltpu.SemaphoreType.DMA((n,)),
                pltpu.SemaphoreType.DMA((n,)),
                pltpu.SemaphoreType.DMA((n * parts_of(nv, own_rows),)),
                pltpu.SemaphoreType.DMA((n * parts_of(nv, own_rows),)),
                pltpu.SemaphoreType.DMA((2, (n - 1) * LAG + 1)),
                pltpu.SemaphoreType.DMA((2, (n - 1) * LAG + 1)),
                pltpu.SemaphoreType.DMA((2, items // tile)),
                pltpu.SemaphoreType.DMA((2, items // tile)),
                pltpu.SemaphoreType.DMA((n * nv,)),
                pltpu.SemaphoreType.DMA((2 * nv,)),
            ],
            compiler_params=pltpu.CompilerParams(
                collective_id=0, has_side_effects=True, vmem_limit_bytes=66_000_000
            ),
        )(hidden, gain, unembed, targets[None, :], seq_ids[None, :])
        split = pl.pallas_call(
            split_outputs,
            out_shape=[jax.ShapeDtypeStruct((1, k), jnp.float32) for k in 3 * [own_rows] + [SEQS]],
            in_specs=[vmem],
            out_specs=[vmem] * 4,
        )(out)
        return tuple(array[0] for array in split)

    return jax.shard_map(
        local,
        mesh=mesh,
        in_specs=(P("width", None), P(), P("width", "vocab"), P(), P()),
        out_specs=(P("width"), P("width"), P("width"), P()),
        check_vma=False,
    )
```
